128 devices in a mesh: stn: 16 (over x, y_lo, core), tm: 8 (over z, y_hi).
Axes of the slice: x: 4, y: 4 (y_hi: 2, y_lo: 2; y = y_hi * 2 + y_lo), z: 4, core: 2. Of those that a mesh axis runs over, the one named last changes fastest.
Arguments:
- samples: bfloat16 [1024, 1048576], P('stn', 'tm'), may hold values from -6 to 6
Outputs:
- visibilities: float32 [128, 2, 1024, 1024], P(('stn', 'tm'))
The draws below stay inside these ranges and needn't reach their ends.
All inputs are finite; a program needn't handle non-finite values.
Results may differ from the reference program's by a relative error of at most 0.0062.
Values may be sent and summed in bfloat16 or wider, within the bound.
A program may use at most 256 MiB of HBM per device.

```python
import jax
import jax.numpy as jnp
from jax import lax

IN_DEV = 64
FRAME = 8192
TAPS = 12
INPUTS = 1024
FRAMES = 128
SAMPLES = 1048576
KEPT = 128
CH_START = 1984
N_STN = 16


def level_of(key, shape, shards, low, high):
    level = 1.0
    for axis_at, parts in shards:
        steps = jax.random.uniform(jax.random.fold_in(jax.random.fold_in(key, 6), axis_at), (parts,), jnp.float32, low / len(shards), high / len(shards))
        level = level * jnp.repeat(jnp.exp(steps), shape[axis_at] // parts).reshape((-1,) + (1,) * (len(shape) - 1 - axis_at))
    return level


def scatter_about(own_key, shape, scale, bound, shards=(), held_as=jnp.bfloat16):
    result = jax.random.normal(own_key, shape, jnp.float32) * scale
    if len(shards) > 0:
        result = level_of(own_key, shape, shards, -0.22, 0.18) * result
    return jnp.clip(result, min=-bound, max=bound).astype(held_as)


def setup_inputs(seed: int = 0) -> dict:
    seeds = jax.random.split(jax.random.key(seed), 2)
    samples = scatter_about(seeds[0], (INPUTS, SAMPLES), 1.0, 6.0, ((0, 16), (1, 8)))
    return dict(samples=samples)


def prototype():
    length = TAPS * FRAME
    place = jnp.arange(length, dtype=jnp.int32).astype(jnp.float32)
    centred = (place - 0.5 * length + 0.5) / FRAME
    window = 0.54 - 0.46 * jnp.cos(2.0 * jnp.pi * place / (length - 1))
    return (jnp.sinc(centred) * window).reshape(TAPS, FRAME)


def transform_table(kept_channels, first_channel):
    sample_index = jnp.arange(FRAME, dtype=jnp.int32)
    column = jnp.arange(2 * kept_channels, dtype=jnp.int32)
    channel = first_channel + column // 2
    phase = (channel[:, None] * sample_index[None, :]) % FRAME
    angle = (2.0 * jnp.pi / FRAME) * phase.astype(jnp.float32)
    scaling = (2.0 / FRAME) ** 0.5
    table = jnp.where((column % 2 == 0)[:, None], jnp.cos(angle), -jnp.sin(angle)) * scaling
    return table.astype(jnp.bfloat16)


def reference(samples):
    prototype_taps = prototype()
    transform = transform_table(KEPT, CH_START)
    margin_frames = TAPS - 1
    grouped = samples.reshape(N_STN, IN_DEV, FRAMES, FRAME)

    def group_spectra(blocks):
        zero_frames = jnp.zeros((IN_DEV, margin_frames, FRAME), blocks.dtype)
        padded = jnp.concatenate([zero_frames, blocks], axis=1)
        running = jnp.zeros((IN_DEV, FRAMES, FRAME), jnp.float32)
        for tap_index in range(TAPS):
            begin = margin_frames - tap_index
            running = running + prototype_taps[tap_index] * padded[:, begin:begin + FRAMES].astype(jnp.float32)
        filtered = running.astype(jnp.bfloat16)
        spectra = lax.dot_general(transform, filtered, (((1,), (2,)), ((), ())),
                                  preferred_element_type=jnp.float32)
        return spectra.astype(jnp.bfloat16)

    spectra_all = lax.map(group_spectra, grouped)

    def correlate(channel):
        picked = lax.dynamic_slice_in_dim(spectra_all, 2 * channel, 2, axis=1)
        ordered = jnp.transpose(picked, (0, 2, 1, 3)).reshape(INPUTS, 2 * FRAMES)
        swapped = jnp.stack([picked[:, 1], -picked[:, 0]], axis=1)
        swapped = jnp.transpose(swapped, (0, 2, 1, 3)).reshape(INPUTS, 2 * FRAMES)
        real_part = jnp.dot(ordered, ordered.T, preferred_element_type=jnp.float32)
        imag_part = jnp.dot(swapped, ordered.T, preferred_element_type=jnp.float32)
        return jnp.stack([real_part, imag_part]) * (1.0 / FRAMES)

    return lax.map(correlate, jnp.arange(KEPT, dtype=jnp.int32))
```

```python
import functools
import numpy as np
import jax
import jax.numpy as jnp
from jax import lax
from jax.experimental import pallas as pl
from jax.experimental.pallas import tpu as pltpu

FRAME = 8192
TAPS = 12
GROUP = 16
OUT = 27
BLK = 1024
QUARTER = FRAME // 4
KEPT = 128
bf = jnp.bfloat16
f32 = jnp.float32


def prototype():
    length = TAPS * FRAME
    place = np.arange(length, dtype=np.float32)
    centred = (place - np.float32(0.5 * length - 0.5)) / np.float32(FRAME)
    window = np.float32(0.54) - np.float32(0.46) * np.cos(2.0 * np.pi * place.astype(np.float64) / (length - 1)).astype(np.float32)
    return (np.sinc(centred.astype(np.float64)).astype(np.float32) * window).reshape(TAPS, FRAME)


def table():
    n = np.arange(QUARTER)
    col = np.arange(128)
    chan = (col % 32) * 4 + col // 32
    phase = (n[:, None] * (chan[None, :] + 1984)) % FRAME
    ang = (np.float32(2.0 * np.pi / FRAME) * phase.astype(np.float32)).astype(np.float64)
    sc = np.float32((2.0 / FRAME) ** 0.5)
    re = np.cos(ang).astype(np.float32) * sc
    im = -np.sin(ang).astype(np.float32) * sc
    return np.concatenate([re, im], axis=1)


ORDER = [0, 11, 1, 10, 2, 9, 3, 8, 4, 7, 5, 6]


def rot(d, q, r, p):
    k = (q * r) % 4
    return [((1, 0), (1, 1)), ((1, 1), (-1, 0)), ((-1, 0), (-1, 1)), ((-1, 1), (1, 0))][k][p]


def kernel_a(*refs, frames):
    x_refs = refs[:frames]
    h_ref, t_ref, out_ref, hrep, filt, acc, slab = refs[frames:]
    out_frames = frames + TAPS - 1
    g = pl.program_id(0)
    i = pl.program_id(1)
    n0 = pl.multiple_of(i * BLK, BLK)

    @pl.when(g == 0)
    def _():
        for k in range(TAPS):
            row = h_ref[k:k + 1, pl.ds(n0, BLK)]
            hrep[k * 8:(k + 1) * 8, pl.ds(n0, BLK)] = jnp.broadcast_to(row, (8, BLK)).astype(bf)

    @pl.when(i == 0)
    def _():
        acc[...] = jnp.zeros_like(acc)

    for j in range(BLK // 256):
        lanes = slice(j * 256, (j + 1) * 256)
        hl = pl.ds(pl.multiple_of(n0 + j * 256, 256), 256)
        hs = [hrep[k * 8:(k + 1) * 8, hl] for k in range(TAPS)]
        for half in range(2):
            rows = slice(half * 8, half * 8 + 8)
            xs = [x[rows, lanes] for x in x_refs]
            for t in range(out_frames):
                s = None
                for k in ORDER:
                    if 0 <= t - k < frames:
                        p = hs[k] * xs[t - k]
                        s = p if s is None else s + p
                filt[t * 16 + half * 8:t * 16 + half * 8 + 8, lanes] = s

    tq = pl.multiple_of((i % (QUARTER // BLK)) * BLK, BLK)
    d = jnp.dot(filt[...], t_ref[pl.ds(tq, BLK), :], preferred_element_type=f32)
    q = i // (QUARTER // BLK)
    for qq in range(4):
        @pl.when(q == qq)
        def _():
            if qq == 0:
                acc[...] += d
            else:
                lane = lax.broadcasted_iota(jnp.int32, (1, 128), 1)
                r = lane // 32
                dre, dim = d[:, :128], d[:, 128:]
                for p in range(2):
                    v = None
                    for rr in range(4):
                        sg, src = rot(None, qq, rr, p)
                        w = (dre, dim)[src]
                        w = w if sg > 0 else -w
                        v = w if v is None else jnp.where(r == rr, w, v)
                    acc[:, p * 128:(p + 1) * 128] += v

    @pl.when(i == pl.num_programs(1) - 1)
    def _():
        for b in range(4):
            lo, hi = b * 128, min((b + 1) * 128, out_frames * 16)
            for p in range(2):
                blk = acc[lo:hi, p * 128:(p + 1) * 128]
                if hi - lo < 128:
                    blk = jnp.concatenate([blk, jnp.zeros((128 - (hi - lo), 128), f32)], axis=0)
                tr = blk.T
                row = (b // 2) * 4 + p * 2 + b % 2
                for r in range(4):
                    slab[pl.ds(r * 8 + row, 32, stride=32), :] = tr[r * 32:(r + 1) * 32]
        out_ref[...] = slab[...].astype(bf)


def run_a(x):
    inputs, samples = x.shape
    frames = samples // FRAME
    steps = FRAME // BLK
    groups = inputs // GROUP
    out_frames = frames + TAPS - 1
    h = jnp.asarray(prototype())
    t = jnp.asarray(table()).astype(bf)
    specs = [pl.BlockSpec((GROUP, BLK), functools.partial(lambda f, g, i: (g, f * steps + i), f)) for f in range(frames)]
    return pl.pallas_call(
        functools.partial(kernel_a, frames=frames),
        grid=(groups, steps),
        in_specs=specs + [pl.BlockSpec(h.shape, lambda g, i: (0, 0)), pl.BlockSpec(t.shape, lambda g, i: (0, 0))],
        out_specs=pl.BlockSpec((None, KEPT * 8, 128), lambda g, i: (g, 0, 0)),
        out_shape=jax.ShapeDtypeStruct((groups, KEPT * 8, 128), bf),
        scratch_shapes=[
            pltpu.VMEM((TAPS * 8, FRAME), bf),
            pltpu.VMEM((out_frames * 16, BLK), bf),
            pltpu.VMEM((out_frames * 16, 256), f32),
            pltpu.VMEM((KEPT * 8, 128), f32),
        ],
        compiler_params=pltpu.CompilerParams(dimension_semantics=("arbitrary", "arbitrary"), vmem_limit_bytes=60 * 2**20),
    )(*([x] * frames), h, t)


def kernel_c(r_ref, out_ref, gmat, gswap, *, stations, blocks, groups):
    depth = 2 * blocks * 16
    scale = 1.0 / (blocks * 16)

    @pl.when(pl.program_id(0) == 0)
    def _():
        row = lax.broadcasted_iota(jnp.int32, (8, 128), 0)
        lane = lax.broadcasted_iota(jnp.int32, (8, 128), 1)

        def station_pair(sp, carry):
            pieces = []
            for sg in range(8):
                s = sp * 2 + sg // 4
                g = sg % 4
                v = [r_ref[g, pl.ds(pl.multiple_of((s * blocks + m) * 8, 8), 8), :].astype(f32) for m in range(blocks)]
                rolled = [pltpu.roll(x, 4, 0) for x in v]
                rows = []
                for m in range(0, blocks, 2):
                    lo = rolled[m - 1] if m > 0 else jnp.zeros_like(v[0])
                    rows.append(v[m] + jnp.where(row < 4, lo, rolled[m + 1]))
                pieces.append(rows)
            for j in range(blocks // 2):
                a = [pieces[sg][j] for sg in range(8)]
                for d in (4, 2, 1):
                    low = (lane // 16) // d % 2 == 0
                    new = list(a)
                    for i in range(8):
                        if i // d % 2 == 0:
                            new[i] = jnp.where(low, a[i], pltpu.roll(a[i + d], 16 * d, 1))
                            new[i + d] = jnp.where(low, pltpu.roll(a[i], 128 - 16 * d, 1), a[i + d])
                    a = new
                cols = pl.ds(pl.multiple_of(sp * 128, 128), 128)
                for t8 in range(8):
                    x = a[t8]
                    k0 = t8 * (blocks * 4) + j * 8
                    gmat[k0:k0 + 8, cols] = x.astype(bf)
                    sw = jnp.where(row % 4 < 2, pltpu.roll(x, 6, 0), -pltpu.roll(x, 2, 0))
                    gswap[k0:k0 + 8, cols] = sw.astype(bf)
            return carry

        lax.fori_loop(0, stations // 2, station_pair, 0)

    rows_out = out_ref.shape[1]
    cols = pl.ds(pl.multiple_of(pl.program_id(0) * rows_out, rows_out), rows_out)
    g = gmat[...]
    dims = (((0,), (0,)), ((), ()))
    out_ref[0] = lax.dot_general(gmat[:, cols], g, dims, preferred_element_type=f32) * scale
    out_ref[1] = lax.dot_general(gswap[:, cols], g, dims, preferred_element_type=f32) * scale


def run_c(r, stations=16, blocks=8):
    groups = r.shape[0]
    inputs = stations * groups * GROUP
    depth = 2 * blocks * 16
    tile = 128
    return pl.pallas_call(
        functools.partial(kernel_c, stations=stations, blocks=blocks, groups=groups),
        grid=(inputs // tile,),
        in_specs=[pl.BlockSpec(r.shape, lambda i: (0, 0, 0))],
        out_specs=pl.BlockSpec((None, 2, tile, inputs), lambda i: (0, 0, i, 0)),
        out_shape=jax.ShapeDtypeStruct((1, 2, inputs, inputs), f32),
        scratch_shapes=[pltpu.VMEM((depth, inputs), bf), pltpu.VMEM((depth, inputs), bf)],
        compiler_params=pltpu.CompilerParams(dimension_semantics=("arbitrary",), vmem_limit_bytes=40 * 2**20),
    )(r)


def on_device(samples):
    stations = lax.axis_size("stn")
    blocks = lax.axis_size("tm")
    sent = run_a(samples)
    groups = sent.shape[0]
    devices = stations * blocks
    got = lax.all_to_all(
        sent.reshape(groups, devices, 8, 128), ("stn", "tm"), split_axis=1, concat_axis=1, tiled=True
    )
    return run_c(got.reshape(groups, devices * 8, 128), stations, blocks)


def solution(mesh):
    return jax.shard_map(
        on_device,
        mesh=mesh,
        in_specs=(jax.sharding.PartitionSpec("stn", "tm"),),
        out_specs=jax.sharding.PartitionSpec(("stn", "tm"), None, None, None),
        check_vma=False,
    )
```
